1024 devices in a mesh: row: 16 (over z, core), col: 64 (over y, x).
Axes of the slice: x: 8, y: 8, z: 8, core: 2. Of those that a mesh axis runs over, the one named last changes fastest.
Arguments:
- gate_pre: bfloat16 [4096, 16384], P('row', 'col'), may hold values from -8 to 8
- up_pre: bfloat16 [4096, 16384], P('row', 'col'), may hold values from -6 to 6
- down_t: bfloat16 [4096, 16384], P('row', 'col'), may hold values from -0.09375 to 0.09375
- grad_out: bfloat16 [4096, 4096], P('row', 'col'), may hold values from -16 to 16
Outputs:
- gate_grad: bfloat16 [4096, 16384], P('row', 'col')
- up_grad: bfloat16 [4096, 16384], P('row', 'col')
- weight_grad: bfloat16 [4096, 16384], P('row', 'col')
The draws below stay inside these ranges and needn't reach their ends.
All inputs are finite; a program needn't handle non-finite values.
Results may differ from the reference program's by a relative error of at most 0.0049.
Values may be sent and summed in bfloat16 or wider, within the bound.
A program may use at most 32 MiB of HBM per device.

```python
import jax
import jax.numpy as jnp

D = 4096
FF = 16384
TOKENS = 4096


def raised(drawn, own_key, source, target, shards_of, factor):
    owner, partner = [(jnp.arange(drawn.shape[axis_at]) // (drawn.shape[axis_at] // shards_of)).reshape([-1 if axis == axis_at else 1 for axis in range(drawn.ndim)]) for axis_at in (source, target)]
    chosen = jax.random.permutation(own_key, shards_of)[partner]
    strong = (owner == chosen) | (owner == (partner + shards_of // 2) % shards_of)
    return jnp.where(strong, factor * drawn, drawn)


def block_scale(own_key, dims, pieces, least, largest):
    def one(dim, shards_of):
        heights = jax.random.uniform(jax.random.fold_in(jax.random.fold_in(own_key, 6), dim), (shards_of,), jnp.float32, least / len(pieces), largest / len(pieces))
        return jnp.repeat(jnp.exp(heights), dims[dim] // shards_of).reshape((-1,) + (1,) * (len(dims) - dim - 1))

    gain = one(*pieces[0])
    for cut in pieces[1:]:
        gain = gain * one(*cut)
    return gain


def normal_values(stream_key, dims, deviation, reach, pieces=(), held_as=jnp.bfloat16):
    entries = jax.random.normal(stream_key, dims, jnp.float32) * deviation
    if len(pieces) > 0:
        entries = block_scale(stream_key, dims, pieces, -0.22, 0.18) * entries
    return jnp.clip(entries, min=-reach, max=reach).astype(held_as)


def noise_with(stream_key, shape, spread, reach, shards, heavy, kind=jnp.bfloat16):
    values = spread * jax.random.normal(stream_key, shape, jnp.float32)
    if shards:
        values = values * block_scale(stream_key, shape, shards, -0.22, 0.18)
    return jnp.clip(raised(values, jax.random.fold_in(stream_key, 3), *heavy), -reach, reach).astype(kind)


def setup_inputs(seed: int = 0) -> dict:
    key_of = jax.random.split(jax.random.key(seed), 5)
    gate_pre = normal_values(key_of[0], (TOKENS, FF), 1.5, 8.0, ((0, 16), (1, 64)))
    up_pre = normal_values(key_of[1], (TOKENS, FF), 1.0, 6.0, ((0, 16), (1, 64)))
    down_t = normal_values(key_of[2], (D, FF), D ** -0.5, 0.09375, ((0, 16), (1, 64)))
    grad_out = noise_with(key_of[3], (TOKENS, D), 1.0, 16.0, ((0, 16), (1, 64)), (0, 1, 64, 4.0))
    return dict(gate_pre=gate_pre, up_pre=up_pre, down_t=down_t, grad_out=grad_out)


def reference(gate_pre, up_pre, down_t, grad_out):
    gate_value = gate_pre.astype(jnp.float32)
    up_value = up_pre.astype(jnp.float32)
    gate_sigmoid = jax.nn.sigmoid(gate_value)
    activated = gate_value * gate_sigmoid
    hidden = (activated * up_value).astype(jnp.bfloat16)
    hidden_grad = jnp.dot(grad_out, down_t, preferred_element_type=jnp.float32)
    weight_sum = jnp.dot(grad_out.T, hidden, preferred_element_type=jnp.float32)
    weight_grad = (weight_sum * (TOKENS ** -0.5)).astype(jnp.bfloat16)
    up_grad = (hidden_grad * activated).astype(jnp.bfloat16)
    slope = gate_sigmoid * (1.0 + gate_value * (1.0 - gate_sigmoid))
    gate_grad = (hidden_grad * up_value * slope).astype(jnp.bfloat16)
    return gate_grad, up_grad, weight_grad
```

```python
import jax
import jax.numpy as jnp
from jax import lax
from jax.experimental import pallas as pl
from jax.experimental.pallas import tpu as pltpu
from jax.sharding import PartitionSpec as P

N = 8
BF = jnp.bfloat16
F32 = jnp.float32


def md(v):
    return lax.rem(v + 2 * N, N)


def kernel(
    gate_ref,
    up_ref,
    down_ref,
    go_ref,
    ggrad_ref,
    ugrad_ref,
    wgrad_ref,
    gt,
    gp,
    wf,
    hid,
    act,
    ups,
    part,
    got,
    hg,
    a1,
    b1,
    a2r,
    a2l,
    b2r,
    b2l,
    pa,
    pb,
    wr,
    wl,
    wp,
    hp,
    rs,
    s1,
    s2,
    sp,
    sb,
    sw,
    swp,
    sh,
    srs,
):
    row, col = lax.axis_index("row"), lax.axis_index("col")
    z, c = lax.div(row, 2), lax.rem(row, 2)
    y, x = lax.div(col, N), lax.rem(col, N)
    cp = 1 - c

    def at_x(v):
        return {"row": row, "col": y * N + v}

    def at_y(v):
        return {"row": row, "col": v * N + x}

    def at_z(v):
        return {"row": v * 2 + c, "col": col}

    partner = {"row": z * 2 + cp, "col": col}

    def send(ref, dst, ssem, rsem, dev):
        pltpu.make_async_remote_copy(
            src_ref=ref, dst_ref=dst, send_sem=ssem, recv_sem=rsem, device_id=dev
        ).start()

    def arrived(ref, sem):
        pltpu.make_async_copy(ref, ref, sem).wait()

    barrier = pltpu.get_barrier_semaphore()
    for k in range(1, N):
        pl.semaphore_signal(barrier, inc=1, device_id=at_x(md(x + k)))
        pl.semaphore_signal(barrier, inc=1, device_id=at_y(md(y + k)))
        pl.semaphore_signal(barrier, inc=1, device_id=at_z(md(z + k)))
    pl.semaphore_signal(barrier, inc=1, device_id=partner)

    eye = (
        lax.broadcasted_iota(jnp.int32, (64, 64), 0)
        == lax.broadcasted_iota(jnp.int32, (64, 64), 1)
    ).astype(BF)
    gt[y, x] = lax.dot_general(
        eye, go_ref[...], (((1,), (1,)), ((), ())), preferred_element_type=F32
    ).astype(BF)
    wf[z, c] = down_ref[...]

    pl.semaphore_wait(barrier, 3 * (N - 1) + 1)

    own_a = gt.at[y, x, pl.ds(0, 32)]
    own_b = gt.at[y, x, pl.ds(32, 32)]
    for k in (4, 3, 5, 2, 6, 1, 7):
        send(own_a, own_a, s1, a1.at[k], at_x(md(x + k)))
        send(own_b, own_b, s1, b1.at[k], at_y(md(y + k)))

    def w_ref(v, half=None):
        return wf.at[v, c] if half is None else wf.at[v, c, pl.ds(128 * half, 128)]

    def w_step(s):
        right = w_ref(md(z - s), 0 if s == 3 else None)
        left = w_ref(md(z + s), 1 if s == 3 else None)
        if s > 0:
            full_r, full_l = w_ref(md(z - s)), w_ref(md(z + s))
            arrived(full_r, wr.at[s - 1])
            send(right, right, sw, wr.at[s], at_z(md(z + 1)))
            arrived(full_l, wl.at[s - 1])
            send(left, left, sw, wl.at[s], at_z(md(z - 1)))
            send(full_r, full_r, swp, wp, partner)
            send(full_l, full_l, swp, wp, partner)
        else:
            send(right, right, sw, wr.at[s], at_z(md(z + 1)))
            send(left, left, sw, wl.at[s], at_z(md(z - 1)))
            send(right, right, swp, wp, partner)

    w_step(0)

    gate = gate_ref[...].astype(F32)
    up = up_ref[...].astype(F32)
    sig = jax.nn.sigmoid(gate)
    activated = gate * sig
    act[...] = activated
    ups[...] = up * (sig * (1.0 + gate * (1.0 - sig)))
    hid[0] = (activated * up).astype(BF)
    send(hid.at[0], hid.at[1], sh, hp, partner)

    def a_ref(v, h):
        return gt.at[v, pl.ds(4 * h, 4), pl.ds(0, 32)]

    def b_ref(v, h):
        return gt.at[pl.ds(4 * h, 4), v, pl.ds(32, 32)]

    def ring(s, h):
        if not (s == 3 and h == 1):
            ra, rb = a_ref(md(y - s), h), b_ref(md(x - s), h)
            if s > 0:
                arrived(ra, a2r.at[s - 1, h])
            send(ra, ra, s2, a2r.at[s, h], at_y(md(y + 1)))
            if s > 0:
                arrived(rb, b2r.at[s - 1, h])
            send(rb, rb, s2, b2r.at[s, h], at_x(md(x + 1)))
        elif s == 3:
            ra, rb = a_ref(md(y - s), h), b_ref(md(x - s), h)
            arrived(ra, a2r.at[s - 1, h])
            arrived(rb, b2r.at[s - 1, h])
        la, lb = a_ref(md(y + s), h), b_ref(md(x + s), h)
        if s > 0:
            arrived(la, a2l.at[s - 1, h])
        if not (s == 3 and h == 0):
            send(la, la, s2, a2l.at[s, h], at_y(md(y - 1)))
        if s > 0:
            arrived(lb, b2l.at[s - 1, h])
        if not (s == 3 and h == 0):
            send(lb, lb, s2, b2l.at[s, h], at_x(md(x - 1)))

    def share(j, yv, xv):
        theirs = gt.at[yv, pl.ds(4 * cp, 4), pl.ds(0, 32)]
        send(theirs, gp.at[yv, slice(None), pl.ds(0, 32)], sp, pa.at[j], partner)

        @pl.when(lax.div(xv, 4) == cp)
        def _():
            send(
                gt.at[slice(None), xv, pl.ds(32, 32)],
                gp.at[slice(None), lax.rem(xv, 4), pl.ds(32, 32)],
                sb,
                pb.at[j],
                partner,
            )

    def reduce(j, yv, xv):
        mine = gp.at[yv, slice(None), pl.ds(0, 32)]
        arrived(mine, pa.at[j])
        total = jnp.dot(
            gt[yv, pl.ds(4 * c, 4), pl.ds(0, 32)].reshape(128, 256),
            hid[0],
            preferred_element_type=F32,
        ) + jnp.dot(
            gp[yv, :, pl.ds(0, 32)].reshape(128, 256),
            hid[1],
            preferred_element_type=F32,
        )
        part[yv, :, pl.ds(0, 32)] = total.astype(BF).reshape(4, 32, 256)
        away = md(yv - z)

        @pl.when(away != 0)
        def _():
            send(
                part.at[yv, slice(None), pl.ds(0, 32)],
                got.at[away - 1, slice(None), pl.ds(0, 32)],
                srs,
                rs,
                at_z(yv),
            )

        @pl.when(lax.div(xv, 4) == c)
        def _():
            xi = lax.rem(xv, 4)
            arrived(gp.at[slice(None), xi, pl.ds(32, 32)], pb.at[j])
            total_b = jnp.dot(
                gt[:, xv, pl.ds(32, 32)].reshape(256, 256),
                hid[0],
                preferred_element_type=F32,
            ) + jnp.dot(
                gp[:, xi, pl.ds(32, 32)].reshape(256, 256),
                hid[1],
                preferred_element_type=F32,
            )
            part[:, xi, pl.ds(32, 32)] = total_b.astype(BF).reshape(N, 32, 256)
            for k in (4, 3, 5, 2, 6, 1, 7):
                send(
                    part.at[md(z + k), xi, pl.ds(32, 32)],
                    got.at[k - 1, xi, pl.ds(32, 32)],
                    srs,
                    rs,
                    at_z(md(z + k)),
                )

    for k in range(1, N):
        arrived(gt.at[y, md(x - k), pl.ds(0, 32)], a1.at[k])
        arrived(gt.at[md(y - k), x, pl.ds(32, 32)], b1.at[k])
    ring(0, 0)
    ring(0, 1)
    share(0, y, x)
    arrived(hid.at[1], hp)
    ring(1, 0)
    ring(1, 1)
    share(1, md(y - 1), md(x - 1))
    share(2, md(y + 1), md(x + 1))
    reduce(0, y, x)
    w_step(1)
    ring(2, 0)
    ring(2, 1)
    share(3, md(y - 2), md(x - 2))
    share(4, md(y + 2), md(x + 2))
    reduce(1, md(y - 1), md(x - 1))
    reduce(2, md(y + 1), md(x + 1))
    w_step(2)
    ring(3, 0)
    ring(3, 1)
    share(5, md(y - 3), md(x - 3))
    share(6, md(y + 3), md(x + 3))
    reduce(3, md(y - 2), md(x - 2))
    reduce(4, md(y + 2), md(x + 2))
    w_step(3)
    arrived(a_ref(md(y + 4), 0), a2r.at[3, 0])
    arrived(a_ref(md(y + 4), 1), a2l.at[3, 1])
    arrived(b_ref(md(x + 4), 0), b2r.at[3, 0])
    arrived(b_ref(md(x + 4), 1), b2l.at[3, 1])
    share(7, md(y + 4), md(x + 4))
    reduce(5, md(y - 3), md(x - 3))
    reduce(6, md(y + 3), md(x + 3))
    reduce(7, md(y + 4), md(x + 4))
    far = md(z + 4)
    arrived(w_ref(far, 0), wr.at[3])
    arrived(w_ref(far, 1), wl.at[3])
    send(w_ref(far), w_ref(far), swp, wp, partner)
    arrived(wf.at[slice(None), cp], wp)

    hg[...] = jnp.zeros_like(hg)

    @pl.loop(0, N)
    def _(v):
        both = gt[v].reshape(512, 256)
        hg[...] += lax.dot_general(
            both,
            wf[v].reshape(512, 256),
            (((0,), (0,)), ((), ())),
            preferred_element_type=F32,
        )

    ugrad_ref[...] = (hg[...] * act[...]).astype(BF)
    ggrad_ref[...] = (hg[...] * ups[...]).astype(BF)

    own = jnp.dot(
        gt[z, pl.ds(4 * c, 4)].reshape(256, 256), hid[0], preferred_element_type=F32
    ) + jnp.dot(gp[z].reshape(256, 256), hid[1], preferred_element_type=F32)

    arrived(gt.at[slice(0, 7), slice(0, 1)], s1)
    arrived(gt.at[slice(0, 7)], s2)
    arrived(gp.at[slice(None), slice(None), pl.ds(0, 32)], sp)
    arrived(gp.at[slice(None), slice(None), pl.ds(32, 32)], sb)
    arrived(wf.at[slice(0, 7), 0], sw)
    arrived(wf.at[slice(None), 0], swp)
    arrived(hid.at[0], sh)
    arrived(got, srs)
    arrived(got, rs)
    total = own
    for k in range(N - 1):
        total = total + got[k].reshape(256, 256).astype(F32)
    wgrad_ref[...] = (total * (1.0 / 64.0)).astype(BF)


def per_device(gate_pre, up_pre, down_t, grad_out):
    vmem = pl.BlockSpec(memory_space=pltpu.VMEM)
    block = jax.ShapeDtypeStruct((256, 256), BF)
    dma = pltpu.SemaphoreType.DMA
    return pl.pallas_call(
        kernel,
        out_shape=(block, block, block),
        in_specs=[vmem] * 4,
        out_specs=(vmem, vmem, vmem),
        scratch_shapes=[
            pltpu.VMEM((N, N, 64, 256), BF),
            pltpu.VMEM((N, 4, 64, 256), BF),
            pltpu.VMEM((N, 2, 256, 256), BF),
            pltpu.VMEM((2, 256, 256), BF),
            pltpu.VMEM((256, 256), F32),
            pltpu.VMEM((256, 256), F32),
            pltpu.VMEM((N, 4, 64, 256), BF),
            pltpu.VMEM((N - 1, 4, 64, 256), BF),
            pltpu.VMEM((256, 256), F32),
            dma((N,)),
            dma((N,)),
            dma((4, 2)),
            dma((4, 2)),
            dma((4, 2)),
            dma((4, 2)),
            dma((N,)),
            dma((N,)),
            dma((4,)),
            dma((4,)),
            dma,
            dma,
            dma,
            dma,
            dma,
            dma,
            dma,
            dma,
            dma,
            dma,
            dma,
        ],
        compiler_params=pltpu.CompilerParams(
            collective_id=0, has_side_effects=True, vmem_limit_bytes=40 << 20
        ),
    )(gate_pre, up_pre, down_t, grad_out)


def solution(mesh):
    spec = P("row", "col")
    return jax.shard_map(
        per_device,
        mesh=mesh,
        in_specs=(spec, spec, spec, spec),
        out_specs=(spec, spec, spec),
        check_vma=False,
    )
```

```python
import jax
import jax.numpy as jnp
from jax import lax
from jax.experimental import pallas as pl
from jax.experimental.pallas import tpu as pltpu
from jax.sharding import PartitionSpec as P

N = 8
BF = jnp.bfloat16
F32 = jnp.float32


def md(v):
    return lax.rem(v + 2 * N, N)


def kernel(
    gate_hbm,
    up_hbm,
    down_hbm,
    go_hbm,
    ggrad_ref,
    ugrad_ref,
    wgrad_ref,
    gt,
    gp,
    wf,
    hid,
    act,
    ups,
    part,
    got,
    m3,
    m4,
    hg,
    gate_ref,
    up_ref,
    a1,
    b1,
    a2r,
    a2l,
    b2r,
    b2l,
    pa,
    pb,
    w1,
    w2,
    w3,
    w4,
    wp,
    hp,
    rs,
    m3a,
    m4a,
    m3b,
    m4b,
    s1,
    s2,
    sp,
    sb,
    sw,
    swp,
    sh,
    srs,
    loc,
):
    row, col = lax.axis_index("row"), lax.axis_index("col")
    z, c = lax.div(row, 2), lax.rem(row, 2)
    y, x = lax.div(col, N), lax.rem(col, N)
    cp = 1 - c

    def at_x(v):
        return {"row": row, "col": y * N + v}

    def at_y(v):
        return {"row": row, "col": v * N + x}

    def at_z(v):
        return {"row": v * 2 + c, "col": col}

    partner = {"row": z * 2 + cp, "col": col}

    def send(ref, dst, ssem, rsem, dev):
        pltpu.make_async_remote_copy(
            src_ref=ref, dst_ref=dst, send_sem=ssem, recv_sem=rsem, device_id=dev
        ).start()

    def arrived(ref, sem):
        pltpu.make_async_copy(ref, ref, sem).wait()

    barrier = pltpu.get_barrier_semaphore()
    for k in range(1, N):
        pl.semaphore_signal(barrier, inc=1, device_id=at_x(md(x + k)))
        pl.semaphore_signal(barrier, inc=1, device_id=at_y(md(y + k)))
        pl.semaphore_signal(barrier, inc=1, device_id=at_z(md(z + k)))
    pl.semaphore_signal(barrier, inc=1, device_id=partner)

    loads = [
        pltpu.make_async_copy(go_hbm, gt.at[y, x], loc.at[0]),
        pltpu.make_async_copy(down_hbm, wf.at[z, c], loc.at[1]),
        pltpu.make_async_copy(gate_hbm, gate_ref, loc.at[2]),
        pltpu.make_async_copy(up_hbm, up_ref, loc.at[3]),
    ]
    for load in loads:
        load.start()
    loads[0].wait()
    loads[1].wait()

    pl.semaphore_wait(barrier, 3 * (N - 1) + 1)

    own_a = gt.at[y, x, pl.ds(0, 32)]
    own_b = gt.at[y, x, pl.ds(32, 32)]
    for k in (4, 3, 5, 2, 6, 1, 7):
        send(own_a, own_a, s1, a1.at[k], at_x(md(x + k)))
        send(own_b, own_b, s1, b1.at[k], at_y(md(y + k)))

    def w_ref(v, half=None):
        return wf.at[v, c] if half is None else wf.at[v, c, pl.ds(128 * half, 128)]

    def w_share(v):
        send(w_ref(v), w_ref(v), swp, wp, partner)

    def w_first():
        mine = w_ref(z)
        for d, way in ((0, 1), (1, -1)):
            send(mine, mine, sw, w2.at[d], at_z(md(z + 2 * way)))
            send(mine, mine, sw, w1.at[d], at_z(md(z + way)))
        w_share(z)

    def w_second():
        for d, way in ((0, 1), (1, -1)):
            near, far = md(z - way), md(z - 2 * way)
            arrived(w_ref(far), w2.at[d])
            send(w_ref(far), w_ref(far), sw, w3.at[d], at_z(md(z + way)))
            send(w_ref(far, d), w_ref(far, d), sw, w4.at[d], at_z(md(z + 2 * way)))
            arrived(w_ref(near), w1.at[d])
            w_share(far)
            w_share(near)

    def w_last():
        for d, way in ((0, 1), (1, -1)):
            v = md(z - 3 * way)
            arrived(w_ref(v), w3.at[d])
            w_share(v)
        for d in (0, 1):
            arrived(w_ref(md(z + 4), d), w4.at[d])
        w_share(md(z + 4))

    w_first()

    loads[2].wait()
    loads[3].wait()
    gate = gate_ref[...].astype(F32)
    up = up_ref[...].astype(F32)
    sig = jax.nn.sigmoid(gate)
    activated = gate * sig
    act[...] = activated
    ups[...] = up * (sig * (1.0 + gate * (1.0 - sig)))
    hid[0] = (activated * up).astype(BF)
    send(hid.at[0], hid.at[1], sh, hp, partner)

    def a_ref(v, h):
        return gt.at[v, pl.ds(4 * h, 4), pl.ds(0, 32)]

    def b_ref(v, h):
        return gt.at[pl.ds(4 * h, 4), v, pl.ds(32, 32)]

    def ring(s, h):
        if not (s == 3 and h == 1):
            ra, rb = a_ref(md(y - s), h), b_ref(md(x - s), h)
            if s > 0:
                arrived(ra, a2r.at[s - 1, h])
            send(ra, ra, s2, a2r.at[s, h], at_y(md(y + 1)))
            if s > 0:
                arrived(rb, b2r.at[s - 1, h])
            send(rb, rb, s2, b2r.at[s, h], at_x(md(x + 1)))
        elif s == 3:
            ra, rb = a_ref(md(y - s), h), b_ref(md(x - s), h)
            arrived(ra, a2r.at[s - 1, h])
            arrived(rb, b2r.at[s - 1, h])
        la, lb = a_ref(md(y + s), h), b_ref(md(x + s), h)
        if s > 0:
            arrived(la, a2l.at[s - 1, h])
        if not (s == 3 and h == 0):
            send(la, la, s2, a2l.at[s, h], at_y(md(y - 1)))
        if s > 0:
            arrived(lb, b2l.at[s - 1, h])
        if not (s == 3 and h == 0):
            send(lb, lb, s2, b2l.at[s, h], at_x(md(x - 1)))

    def share(j, yv, xv):
        theirs = gt.at[yv, pl.ds(4 * cp, 4), pl.ds(0, 32)]
        send(theirs, gp.at[yv, slice(None), pl.ds(0, 32)], sp, pa.at[j], partner)

        @pl.when(lax.div(xv, 4) == cp)
        def _():
            send(
                gt.at[slice(None), xv, pl.ds(32, 32)],
                gp.at[slice(None), lax.rem(xv, 4), pl.ds(32, 32)],
                sb,
                pb.at[j],
                partner,
            )

    def reduce(j, yv, xv):
        mine = gp.at[yv, slice(None), pl.ds(0, 32)]
        arrived(mine, pa.at[j])
        total = jnp.dot(
            gt[yv, pl.ds(4 * c, 4), pl.ds(0, 32)].reshape(128, 256),
            hid[0],
            preferred_element_type=F32,
        ) + jnp.dot(
            gp[yv, :, pl.ds(0, 32)].reshape(128, 256),
            hid[1],
            preferred_element_type=F32,
        )
        part[yv, :, pl.ds(0, 32)] = total.astype(BF).reshape(4, 32, 256)
        o = md(yv - z)
        d = lax.div(o, 4)
        toward = at_z(md(z + 1 - 2 * d))
        rows = part.at[yv, slice(None), pl.ds(0, 32)]

        @pl.when(jnp.logical_or(o == 1, o == 7))
        def _():
            send(rows, got.at[d, slice(None), pl.ds(0, 32)], srs, rs, toward)

        @pl.when(jnp.logical_or(o == 3, o == 5))
        def _():
            send(rows, m3.at[d, slice(None), pl.ds(0, 32)], srs, m3a.at[d], toward)

        @pl.when(o == 4)
        def _():
            for e, way in ((0, 1), (1, -1)):
                send(
                    part.at[yv, slice(None), pl.ds(16 * e, 16)],
                    m4.at[e, slice(None), pl.ds(0, 16)],
                    srs,
                    m4a.at[e],
                    at_z(md(z + 2 * way)),
                )

        @pl.when(lax.div(xv, 4) == c)
        def _():
            xi = lax.rem(xv, 4)
            arrived(gp.at[slice(None), xi, pl.ds(32, 32)], pb.at[j])
            total_b = jnp.dot(
                gt[:, xv, pl.ds(32, 32)].reshape(256, 256),
                hid[0],
                preferred_element_type=F32,
            ) + jnp.dot(
                gp[:, xi, pl.ds(32, 32)].reshape(256, 256),
                hid[1],
                preferred_element_type=F32,
            )
            part[:, xi, pl.ds(32, 32)] = total_b.astype(BF).reshape(N, 32, 256)
            for e, way in ((0, 1), (1, -1)):
                send(
                    part.at[md(z + 4), xi, pl.ds(32 + 16 * e, 16)],
                    m4.at[e, xi, pl.ds(16, 16)],
                    srs,
                    m4b.at[e, xi],
                    at_z(md(z + 2 * way)),
                )
                send(
                    part.at[md(z + 3 * way), xi, pl.ds(32, 32)],
                    m3.at[e, xi, pl.ds(32, 32)],
                    srs,
                    m3b.at[e, xi],
                    at_z(md(z + way)),
                )
            for e, way in ((0, 1), (1, -1)):
                send(
                    part.at[md(z + way), xi, pl.ds(32, 32)],
                    got.at[e, xi, pl.ds(32, 32)],
                    srs,
                    rs,
                    at_z(md(z + way)),
                )

    def pass_on(yv, xv):
        o = md(yv - z)

        @pl.when(jnp.logical_or(o == 2, o == 6))
        def _():
            d = lax.div(o, 4)
            arrived(m3.at[d, slice(None), pl.ds(0, 32)], m3a.at[d])
            arrived(m4.at[d, slice(None), pl.ds(0, 16)], m4a.at[d])
            summed = part[yv, :, pl.ds(0, 32)].astype(F32) + m3[
                d, :, pl.ds(0, 32)
            ].astype(F32)
            lower = m4[d, :, pl.ds(0, 16)].astype(F32)
            first = (d == 0).astype(F32)
            summed = summed + jnp.concatenate(
                [lower * first, lower * (1.0 - first)], axis=1
            )
            part[yv, :, pl.ds(0, 32)] = summed.astype(BF)
            send(
                part.at[yv, slice(None), pl.ds(0, 32)],
                got.at[2 + d, slice(None), pl.ds(0, 32)],
                srs,
                rs,
                at_z(yv),
            )

        @pl.when(lax.div(xv, 4) == c)
        def _():
            xi = lax.rem(xv, 4)
            for e, way in ((0, 1), (1, -1)):
                v = md(z + 2 * way)
                arrived(m3.at[e, xi, pl.ds(32, 32)], m3b.at[e, xi])
                arrived(m4.at[e, xi, pl.ds(16, 16)], m4b.at[e, xi])
                for h in (0, 1):
                    at = pl.ds(32 + 16 * h, 16)
                    summed = part[v, xi, at].astype(F32) + m3[e, xi, at].astype(F32)
                    if h == e:
                        summed = summed + m4[e, xi, pl.ds(16, 16)].astype(F32)
                    part[v, xi, at] = summed.astype(BF)
                send(
                    part.at[v, xi, pl.ds(32, 32)],
                    got.at[2 + e, xi, pl.ds(32, 32)],
                    srs,
                    rs,
                    at_z(v),
                )

    for k in range(1, N):
        arrived(gt.at[y, md(x - k), pl.ds(0, 32)], a1.at[k])
        arrived(gt.at[md(y - k), x, pl.ds(32, 32)], b1.at[k])
    spots = [(y, x)]
    for k in (1, 2, 3):
        spots.append((md(y - k), md(x - k)))
        spots.append((md(y + k), md(x + k)))
    spots.append((md(y + 4), md(x + 4)))

    ring(0, 0)
    ring(0, 1)
    share(0, *spots[0])
    arrived(hid.at[1], hp)
    reduce(0, *spots[0])
    ring(1, 0)
    ring(1, 1)
    share(1, *spots[1])
    share(2, *spots[2])
    w_second()
    reduce(1, *spots[1])
    reduce(2, *spots[2])
    ring(2, 0)
    ring(2, 1)
    share(3, *spots[3])
    share(4, *spots[4])
    reduce(3, *spots[3])
    reduce(4, *spots[4])
    ring(3, 0)
    ring(3, 1)
    share(5, *spots[5])
    share(6, *spots[6])
    w_last()
    reduce(5, *spots[5])
    reduce(6, *spots[6])
    arrived(a_ref(md(y + 4), 0), a2r.at[3, 0])
    arrived(a_ref(md(y + 4), 1), a2l.at[3, 1])
    arrived(b_ref(md(x + 4), 0), b2r.at[3, 0])
    arrived(b_ref(md(x + 4), 1), b2l.at[3, 1])
    share(7, *spots[7])
    reduce(7, *spots[7])
    pass_on(*spots[0])
    pass_on(*spots[1])
    pass_on(*spots[2])
    pass_on(*spots[3])
    pass_on(*spots[4])
    pass_on(*spots[5])
    pass_on(*spots[6])
    arrived(wf.at[slice(None), cp], wp)

    hg[...] = jnp.zeros_like(hg)

    @pl.loop(0, N)
    def _(v):
        both = gt[v].reshape(512, 256)
        hg[...] += lax.dot_general(
            both,
            wf[v].reshape(512, 256),
            (((0,), (0,)), ((), ())),
            preferred_element_type=F32,
        )

    pass_on(*spots[7])
    ugrad_ref[...] = (hg[...] * act[...]).astype(BF)
    ggrad_ref[...] = (hg[...] * ups[...]).astype(BF)

    own = jnp.dot(
        gt[z, pl.ds(4 * c, 4)].reshape(256, 256), hid[0], preferred_element_type=F32
    ) + jnp.dot(gp[z].reshape(256, 256), hid[1], preferred_element_type=F32)

    arrived(gt.at[slice(0, 7), slice(0, 1)], s1)
    arrived(gt.at[slice(0, 7)], s2)
    arrived(gp.at[slice(None), slice(None), pl.ds(0, 32)], sp)
    arrived(gp.at[slice(None), slice(None), pl.ds(32, 32)], sb)
    arrived(wf.at[slice(0, 7), 0], sw)
    arrived(wf.at[slice(None), 0], swp)
    arrived(hid.at[0], sh)
    arrived(part.at[slice(0, 7)], srs)
    arrived(got, rs)
    total = own
    for k in range(4):
        total = total + got[k].reshape(256, 256).astype(F32)
    wgrad_ref[...] = (total * (1.0 / 64.0)).astype(BF)


def store(gg_ref, ug_ref, wg_ref, gg_hbm, ug_hbm, wg_hbm, sem):
    copies = [
        pltpu.make_async_copy(gg_ref, gg_hbm, sem.at[0]),
        pltpu.make_async_copy(ug_ref, ug_hbm, sem.at[1]),
        pltpu.make_async_copy(wg_ref, wg_hbm, sem.at[2]),
    ]
    for copy in copies:
        copy.start()
    for copy in copies:
        copy.wait()


def per_device(gate_pre, up_pre, down_t, grad_out):
    vmem = pl.BlockSpec(memory_space=pltpu.VMEM)
    hbm = pl.BlockSpec(memory_space=pltpu.HBM)
    block = jax.ShapeDtypeStruct((256, 256), BF)
    dma = pltpu.SemaphoreType.DMA
    results = pl.pallas_call(
        kernel,
        out_shape=(block, block, block),
        in_specs=[hbm] * 4,
        out_specs=(vmem, vmem, vmem),
        scratch_shapes=[
            pltpu.VMEM((N, N, 64, 256), BF),
            pltpu.VMEM((N, 4, 64, 256), BF),
            pltpu.VMEM((N, 2, 256, 256), BF),
            pltpu.VMEM((2, 256, 256), BF),
            pltpu.VMEM((256, 256), F32),
            pltpu.VMEM((256, 256), F32),
            pltpu.VMEM((N, 4, 64, 256), BF),
            pltpu.VMEM((4, 4, 64, 256), BF),
            pltpu.VMEM((2, 4, 64, 256), BF),
            pltpu.VMEM((2, 4, 32, 256), BF),
            pltpu.VMEM((256, 256), F32),
            pltpu.VMEM((256, 256), BF),
            pltpu.VMEM((256, 256), BF),
            dma((N,)),
            dma((N,)),
            dma((4, 2)),
            dma((4, 2)),
            dma((4, 2)),
            dma((4, 2)),
            dma((N,)),
            dma((N,)),
            dma((2,)),
            dma((2,)),
            dma((2,)),
            dma((2,)),
            dma,
            dma,
            dma,
            dma((2,)),
            dma((2,)),
            dma((2, 4)),
            dma((2, 4)),
            dma,
            dma,
            dma,
            dma,
            dma,
            dma,
            dma,
            dma,
            dma((4,)),
        ],
        compiler_params=pltpu.CompilerParams(
            collective_id=0, has_side_effects=True
        ),
    )(gate_pre, up_pre, down_t, grad_out.T)
    return pl.pallas_call(
        store,
        out_shape=(block, block, block),
        in_specs=[vmem] * 3,
        out_specs=(hbm, hbm, hbm),
        scratch_shapes=[dma((3,))],
    )(*results)


def solution(mesh):
    spec = P("row", "col")
    return jax.shard_map(
        per_device,
        mesh=mesh,
        in_specs=(spec, spec, spec, spec),
        out_specs=(spec, spec, spec),
        check_vma=False,
    )
```

```python
import jax
import jax.numpy as jnp
from jax import lax
from jax.experimental import pallas as pl
from jax.experimental.pallas import tpu as pltpu
from jax.sharding import PartitionSpec as P

N = 8
BF = jnp.bfloat16
F32 = jnp.float32


def md(v):
    return lax.rem(v + 2 * N, N)


def kernel(
    gate_hbm,
    up_hbm,
    down_hbm,
    go_hbm,
    ggrad_ref,
    ugrad_ref,
    wgrad_ref,
    gt,
    gp,
    wf,
    hid,
    act,
    ups,
    part,
    got,
    m3,
    m4,
    hg,
    gate_ref,
    up_ref,
    a1,
    b1,
    a2r,
    a2l,
    b2r,
    b2l,
    pa,
    pb,
    w1,
    w2,
    w3,
    w4,
    wp,
    hp,
    rs,
    m3a,
    m4a,
    m3b,
    m4b,
    s1,
    s2,
    sp,
    sb,
    sw,
    swp,
    sh,
    srs,
    loc,
):
    row, col = lax.axis_index("row"), lax.axis_index("col")
    z, c = lax.div(row, 2), lax.rem(row, 2)
    y, x = lax.div(col, N), lax.rem(col, N)
    cp = 1 - c

    def at_x(v):
        return {"row": row, "col": y * N + v}

    def at_y(v):
        return {"row": row, "col": v * N + x}

    def at_z(v):
        return {"row": v * 2 + c, "col": col}

    partner = {"row": z * 2 + cp, "col": col}

    def send(ref, dst, ssem, rsem, dev):
        pltpu.make_async_remote_copy(
            src_ref=ref, dst_ref=dst, send_sem=ssem, recv_sem=rsem, device_id=dev
        ).start()

    def arrived(ref, sem):
        pltpu.make_async_copy(ref, ref, sem).wait()

    barrier = pltpu.get_barrier_semaphore()
    for k in range(1, N):
        pl.semaphore_signal(barrier, inc=1, device_id=at_x(md(x + k)))
        pl.semaphore_signal(barrier, inc=1, device_id=at_y(md(y + k)))
        if k in (1, 2, 6, 7):
            pl.semaphore_signal(barrier, inc=1, device_id=at_z(md(z + k)))
    pl.semaphore_signal(barrier, inc=1, device_id=partner)

    loads = [
        pltpu.make_async_copy(go_hbm, gt.at[y, x], loc.at[0]),
        pltpu.make_async_copy(down_hbm, wf.at[z, c], loc.at[1]),
        pltpu.make_async_copy(gate_hbm, gate_ref, loc.at[2]),
        pltpu.make_async_copy(up_hbm, up_ref, loc.at[3]),
    ]
    for load in loads:
        load.start()
    loads[0].wait()
    loads[1].wait()

    pl.semaphore_wait(barrier, 2 * (N - 1) + 5)

    own_a = gt.at[y, x, pl.ds(0, 32)]
    own_b = gt.at[y, x, pl.ds(32, 32)]
    for k in (4, 3, 5, 2, 6, 1, 7):
        send(own_a, own_a, s1, a1.at[k], at_x(md(x + k)))
        send(own_b, own_b, s1, b1.at[k], at_y(md(y + k)))

    def w_ref(v, half=None):
        return wf.at[v, c] if half is None else wf.at[v, c, pl.ds(128 * half, 128)]

    def w_share(v):
        send(w_ref(v), w_ref(v), swp, wp, partner)

    def w_first():
        mine = w_ref(z)
        for d, way in ((0, 1), (1, -1)):
            send(mine, mine, sw, w2.at[d], at_z(md(z + 2 * way)))
            send(mine, mine, sw, w1.at[d], at_z(md(z + way)))
        w_share(z)

    def w_second():
        for d, way in ((0, 1), (1, -1)):
            near, far = md(z - way), md(z - 2 * way)
            arrived(w_ref(far), w2.at[d])
            send(w_ref(far), w_ref(far), sw, w3.at[d], at_z(md(z + way)))
            send(w_ref(far, d), w_ref(far, d), sw, w4.at[d], at_z(md(z + 2 * way)))
            arrived(w_ref(near), w1.at[d])
            w_share(far)
            w_share(near)

    def w_last():
        for d, way in ((0, 1), (1, -1)):
            v = md(z - 3 * way)
            arrived(w_ref(v), w3.at[d])
            w_share(v)
        for d in (0, 1):
            arrived(w_ref(md(z + 4), d), w4.at[d])
        w_share(md(z + 4))

    w_first()

    loads[2].wait()
    loads[3].wait()
    gate = gate_ref[...].astype(F32)
    up = up_ref[...].astype(F32)
    sig = jax.nn.sigmoid(gate)
    activated = gate * sig
    act[...] = activated
    ups[...] = up * (sig * (1.0 + gate * (1.0 - sig)))
    hid[0] = (activated * up).astype(BF)
    send(hid.at[0], hid.at[1], sh, hp, partner)

    def a_ref(v, h):
        return gt.at[v, pl.ds(4 * h, 4), pl.ds(0, 32)]

    def b_ref(v, h):
        return gt.at[pl.ds(4 * h, 4), v, pl.ds(32, 32)]

    def ring(s, h):
        if not (s == 3 and h == 1):
            ra, rb = a_ref(md(y - s), h), b_ref(md(x - s), h)
            if s > 0:
                arrived(ra, a2r.at[s - 1, h])
            send(ra, ra, s2, a2r.at[s, h], at_y(md(y + 1)))
            if s > 0:
                arrived(rb, b2r.at[s - 1, h])
            send(rb, rb, s2, b2r.at[s, h], at_x(md(x + 1)))
        elif s == 3:
            ra, rb = a_ref(md(y - s), h), b_ref(md(x - s), h)
            arrived(ra, a2r.at[s - 1, h])
            arrived(rb, b2r.at[s - 1, h])
        la, lb = a_ref(md(y + s), h), b_ref(md(x + s), h)
        if s > 0:
            arrived(la, a2l.at[s - 1, h])
        if not (s == 3 and h == 0):
            send(la, la, s2, a2l.at[s, h], at_y(md(y - 1)))
        if s > 0:
            arrived(lb, b2l.at[s - 1, h])
        if not (s == 3 and h == 0):
            send(lb, lb, s2, b2l.at[s, h], at_x(md(x - 1)))

    def share(j, yv, xv):
        theirs = gt.at[yv, pl.ds(4 * cp, 4), pl.ds(0, 32)]
        send(theirs, gp.at[yv, slice(None), pl.ds(0, 32)], sp, pa.at[j], partner)

        @pl.when(lax.div(xv, 4) == cp)
        def _():
            send(
                gt.at[slice(None), xv, pl.ds(32, 32)],
                gp.at[slice(None), lax.rem(xv, 4), pl.ds(32, 32)],
                sb,
                pb.at[j],
                partner,
            )

    def reduce(j, yv, xv):
        mine = gp.at[yv, slice(None), pl.ds(0, 32)]
        arrived(mine, pa.at[j])
        total = jnp.dot(
            gt[yv, pl.ds(4 * c, 4), pl.ds(0, 32)].reshape(128, 256),
            hid[0],
            preferred_element_type=F32,
        ) + jnp.dot(
            gp[yv, :, pl.ds(0, 32)].reshape(128, 256),
            hid[1],
            preferred_element_type=F32,
        )
        part[yv, :, pl.ds(0, 32)] = total.astype(BF).reshape(4, 32, 256)
        o = md(yv - z)
        d = lax.div(o, 4)
        toward = at_z(md(z + 1 - 2 * d))
        rows = part.at[yv, slice(None), pl.ds(0, 32)]

        @pl.when(jnp.logical_or(o == 1, o == 7))
        def _():
            send(rows, got.at[d, slice(None), pl.ds(0, 32)], srs, rs, toward)

        @pl.when(jnp.logical_or(o == 3, o == 5))
        def _():
            send(rows, m3.at[d, slice(None), pl.ds(0, 32)], srs, m3a.at[d], toward)

        @pl.when(o == 4)
        def _():
            for e, way in ((0, 1), (1, -1)):
                send(
                    part.at[yv, slice(None), pl.ds(16 * e, 16)],
                    m4.at[e, slice(None), pl.ds(0, 16)],
                    srs,
                    m4a.at[e],
                    at_z(md(z + 2 * way)),
                )

        @pl.when(lax.div(xv, 4) == c)
        def _():
            xi = lax.rem(xv, 4)
            arrived(gp.at[slice(None), xi, pl.ds(32, 32)], pb.at[j])
            total_b = jnp.dot(
                gt[:, xv, pl.ds(32, 32)].reshape(256, 256),
                hid[0],
                preferred_element_type=F32,
            ) + jnp.dot(
                gp[:, xi, pl.ds(32, 32)].reshape(256, 256),
                hid[1],
                preferred_element_type=F32,
            )
            part[:, xi, pl.ds(32, 32)] = total_b.astype(BF).reshape(N, 32, 256)
            for e, way in ((0, 1), (1, -1)):
                send(
                    part.at[md(z + 4), xi, pl.ds(32 + 16 * e, 16)],
                    m4.at[e, xi, pl.ds(16, 16)],
                    srs,
                    m4b.at[e, xi],
                    at_z(md(z + 2 * way)),
                )
                send(
                    part.at[md(z + 3 * way), xi, pl.ds(32, 32)],
                    m3.at[e, xi, pl.ds(32, 32)],
                    srs,
                    m3b.at[e, xi],
                    at_z(md(z + way)),
                )
            for e, way in ((0, 1), (1, -1)):
                send(
                    part.at[md(z + way), xi, pl.ds(32, 32)],
                    got.at[e, xi, pl.ds(32, 32)],
                    srs,
                    rs,
                    at_z(md(z + way)),
                )

    def pass_on(yv, xv):
        o = md(yv - z)

        @pl.when(jnp.logical_or(o == 2, o == 6))
        def _():
            d = lax.div(o, 4)
            arrived(m3.at[d, slice(None), pl.ds(0, 32)], m3a.at[d])
            arrived(m4.at[d, slice(None), pl.ds(0, 16)], m4a.at[d])
            summed = part[yv, :, pl.ds(0, 32)].astype(F32) + m3[
                d, :, pl.ds(0, 32)
            ].astype(F32)
            lower = m4[d, :, pl.ds(0, 16)].astype(F32)
            first = (d == 0).astype(F32)
            summed = summed + jnp.concatenate(
                [lower * first, lower * (1.0 - first)], axis=1
            )
            part[yv, :, pl.ds(0, 32)] = summed.astype(BF)
            send(
                part.at[yv, slice(None), pl.ds(0, 32)],
                got.at[2 + d, slice(None), pl.ds(0, 32)],
                srs,
                rs,
                at_z(yv),
            )

        @pl.when(lax.div(xv, 4) == c)
        def _():
            xi = lax.rem(xv, 4)
            for e, way in ((0, 1), (1, -1)):
                v = md(z + 2 * way)
                arrived(m3.at[e, xi, pl.ds(32, 32)], m3b.at[e, xi])
                arrived(m4.at[e, xi, pl.ds(16, 16)], m4b.at[e, xi])
                for h in (0, 1):
                    at = pl.ds(32 + 16 * h, 16)
                    summed = part[v, xi, at].astype(F32) + m3[e, xi, at].astype(F32)
                    if h == e:
                        summed = summed + m4[e, xi, pl.ds(16, 16)].astype(F32)
                    part[v, xi, at] = summed.astype(BF)
                send(
                    part.at[v, xi, pl.ds(32, 32)],
                    got.at[2 + e, xi, pl.ds(32, 32)],
                    srs,
                    rs,
                    at_z(v),
                )

    for k in range(1, N):
        arrived(gt.at[y, md(x - k), pl.ds(0, 32)], a1.at[k])
        arrived(gt.at[md(y - k), x, pl.ds(32, 32)], b1.at[k])
    spots = [(y, x)]
    for k in (1, 2, 3):
        spots.append((md(y - k), md(x - k)))
        spots.append((md(y + k), md(x + k)))
    spots.append((md(y + 4), md(x + 4)))

    ring(0, 0)
    ring(0, 1)
    share(0, *spots[0])
    arrived(hid.at[1], hp)
    reduce(0, *spots[0])
    ring(1, 0)
    ring(1, 1)
    share(1, *spots[1])
    share(2, *spots[2])
    w_second()
    reduce(1, *spots[1])
    reduce(2, *spots[2])
    ring(2, 0)
    ring(2, 1)
    share(3, *spots[3])
    share(4, *spots[4])
    reduce(3, *spots[3])
    reduce(4, *spots[4])
    ring(3, 0)
    ring(3, 1)
    share(5, *spots[5])
    share(6, *spots[6])
    w_last()
    reduce(5, *spots[5])
    reduce(6, *spots[6])
    arrived(a_ref(md(y + 4), 0), a2r.at[3, 0])
    arrived(a_ref(md(y + 4), 1), a2l.at[3, 1])
    arrived(b_ref(md(x + 4), 0), b2r.at[3, 0])
    arrived(b_ref(md(x + 4), 1), b2l.at[3, 1])
    share(7, *spots[7])
    reduce(7, *spots[7])
    pass_on(*spots[0])
    pass_on(*spots[1])
    pass_on(*spots[2])
    pass_on(*spots[3])
    pass_on(*spots[4])
    pass_on(*spots[5])
    pass_on(*spots[6])
    arrived(wf.at[slice(None), cp], wp)

    hg[...] = jnp.zeros_like(hg)

    @pl.loop(0, N)
    def _(v):
        both = gt[v].reshape(512, 256)
        hg[...] += lax.dot_general(
            both,
            wf[v].reshape(512, 256),
            (((0,), (0,)), ((), ())),
            preferred_element_type=F32,
        )

    pass_on(*spots[7])
    ugrad_ref[...] = (hg[...] * act[...]).astype(BF)
    ggrad_ref[...] = (hg[...] * ups[...]).astype(BF)

    own = jnp.dot(
        gt[z, pl.ds(4 * c, 4)].reshape(256, 256), hid[0], preferred_element_type=F32
    ) + jnp.dot(gp[z].reshape(256, 256), hid[1], preferred_element_type=F32)

    arrived(gt.at[slice(0, 7), slice(0, 1)], s1)
    arrived(gt.at[slice(0, 7)], s2)
    arrived(gp.at[slice(None), slice(None), pl.ds(0, 32)], sp)
    arrived(gp.at[slice(None), slice(None), pl.ds(32, 32)], sb)
    arrived(wf.at[slice(0, 7), 0], sw)
    arrived(wf.at[slice(None), 0], swp)
    arrived(hid.at[0], sh)
    arrived(part.at[slice(0, 7)], srs)
    arrived(got, rs)
    total = own
    for k in range(4):
        total = total + got[k].reshape(256, 256).astype(F32)
    wgrad_ref[...] = (total * (1.0 / 64.0)).astype(BF)


def store(gg_ref, ug_ref, wg_ref, gg_hbm, ug_hbm, wg_hbm, sem):
    copies = [
        pltpu.make_async_copy(gg_ref, gg_hbm, sem.at[0]),
        pltpu.make_async_copy(ug_ref, ug_hbm, sem.at[1]),
        pltpu.make_async_copy(wg_ref, wg_hbm, sem.at[2]),
    ]
    for copy in copies:
        copy.start()
    for copy in copies:
        copy.wait()


def per_device(gate_pre, up_pre, down_t, grad_out):
    vmem = pl.BlockSpec(memory_space=pltpu.VMEM)
    hbm = pl.BlockSpec(memory_space=pltpu.HBM)
    block = jax.ShapeDtypeStruct((256, 256), BF)
    dma = pltpu.SemaphoreType.DMA
    results = pl.pallas_call(
        kernel,
        out_shape=(block, block, block),
        in_specs=[hbm] * 4,
        out_specs=(vmem, vmem, vmem),
        scratch_shapes=[
            pltpu.VMEM((N, N, 64, 256), BF),
            pltpu.VMEM((N, 4, 64, 256), BF),
            pltpu.VMEM((N, 2, 256, 256), BF),
            pltpu.VMEM((2, 256, 256), BF),
            pltpu.VMEM((256, 256), F32),
            pltpu.VMEM((256, 256), F32),
            pltpu.VMEM((N, 4, 64, 256), BF),
            pltpu.VMEM((4, 4, 64, 256), BF),
            pltpu.VMEM((2, 4, 64, 256), BF),
            pltpu.VMEM((2, 4, 32, 256), BF),
            pltpu.VMEM((256, 256), F32),
            pltpu.VMEM((256, 256), BF),
            pltpu.VMEM((256, 256), BF),
            dma((N,)),
            dma((N,)),
            dma((4, 2)),
            dma((4, 2)),
            dma((4, 2)),
            dma((4, 2)),
            dma((N,)),
            dma((N,)),
            dma((2,)),
            dma((2,)),
            dma((2,)),
            dma((2,)),
            dma,
            dma,
            dma,
            dma((2,)),
            dma((2,)),
            dma((2, 4)),
            dma((2, 4)),
            dma,
            dma,
            dma,
            dma,
            dma,
            dma,
            dma,
            dma,
            dma((4,)),
        ],
        compiler_params=pltpu.CompilerParams(
            collective_id=0, has_side_effects=True, vmem_limit_bytes=56130000
        ),
    )(gate_pre, up_pre, down_t, grad_out.T)
    return pl.pallas_call(
        store,
        out_shape=(block, block, block),
        in_specs=[vmem] * 3,
        out_specs=(hbm, hbm, hbm),
        scratch_shapes=[dma((3,))],
        compiler_params=pltpu.CompilerParams(vmem_limit_bytes=1 << 20),
    )(*results)


def solution(mesh):
    spec = P("row", "col")
    return jax.shard_map(
        per_device,
        mesh=mesh,
        in_specs=(spec, spec, spec, spec),
        out_specs=(spec, spec, spec),
        check_vma=False,
    )
```

```python
import jax
import jax.numpy as jnp
from jax import lax
from jax.experimental import pallas as pl
from jax.experimental.pallas import tpu as pltpu
from jax.sharding import PartitionSpec as P

N = 8
BF = jnp.bfloat16
F32 = jnp.float32


def md(v):
    return lax.rem(v + 2 * N, N)


def kernel(
    gate_hbm,
    up_hbm,
    down_hbm,
    go_hbm,
    ggrad_ref,
    ugrad_ref,
    wgrad_ref,
    gt,
    gp,
    wf,
    hid,
    act,
    ups,
    part,
    got,
    m3,
    m4,
    hg,
    gate_ref,
    up_ref,
    a1,
    b1,
    a2r,
    a2l,
    b2r,
    b2l,
    pa,
    pb,
    w1,
    w2,
    w3,
    w4,
    wp,
    hp,
    rs,
    m3a,
    m4a,
    m3b,
    m4b,
    s1,
    s2,
    sp,
    sb,
    sw,
    swp,
    sh,
    srs,
    loc,
):
    row, col = lax.axis_index("row"), lax.axis_index("col")
    z, c = lax.div(row, 2), lax.rem(row, 2)
    y, x = lax.div(col, N), lax.rem(col, N)
    cp = 1 - c

    def at_x(v):
        return {"row": row, "col": y * N + v}

    def at_y(v):
        return {"row": row, "col": v * N + x}

    def at_z(v):
        return {"row": v * 2 + c, "col": col}

    partner = {"row": z * 2 + cp, "col": col}

    def send(ref, dst, ssem, rsem, dev):
        pltpu.make_async_remote_copy(
            src_ref=ref, dst_ref=dst, send_sem=ssem, recv_sem=rsem, device_id=dev
        ).start()

    def arrived(ref, sem):
        pltpu.make_async_copy(ref, ref, sem).wait()

    barrier = pltpu.get_barrier_semaphore()
    for k in range(1, N):
        pl.semaphore_signal(barrier, inc=1, device_id=at_x(md(x + k)))
        pl.semaphore_signal(barrier, inc=1, device_id=at_y(md(y + k)))
        if k in (1, 2, 6, 7):
            pl.semaphore_signal(barrier, inc=1, device_id=at_z(md(z + k)))
    pl.semaphore_signal(barrier, inc=1, device_id=partner)

    loads = [
        pltpu.make_async_copy(go_hbm, gt.at[y, x], loc.at[0]),
        pltpu.make_async_copy(down_hbm, wf.at[z, c], loc.at[1]),
        pltpu.make_async_copy(gate_hbm, gate_ref, loc.at[2]),
        pltpu.make_async_copy(up_hbm, up_ref, loc.at[3]),
    ]
    for load in loads:
        load.start()
    loads[0].wait()
    loads[1].wait()

    pl.semaphore_wait(barrier, 2 * (N - 1) + 5)

    own_a = gt.at[y, x, pl.ds(0, 32)]
    own_b = gt.at[y, x, pl.ds(32, 32)]
    for k in (4, 3, 5, 2, 6, 1, 7):
        send(own_a, own_a, s1, a1.at[k], at_x(md(x + k)))
        send(own_b, own_b, s1, b1.at[k], at_y(md(y + k)))

    def w_ref(v, half=None):
        return wf.at[v, c] if half is None else wf.at[v, c, pl.ds(128 * half, 128)]

    def w_share(v):
        send(w_ref(v), w_ref(v), swp, wp, partner)

    def w_first():
        mine = w_ref(z)
        for d, way in ((0, 1), (1, -1)):
            send(mine, mine, sw, w2.at[d], at_z(md(z + 2 * way)))
            send(mine, mine, sw, w1.at[d], at_z(md(z + way)))
        w_share(z)

    def w_second():
        for d, way in ((0, 1), (1, -1)):
            near, far = md(z - way), md(z - 2 * way)
            arrived(w_ref(far), w2.at[d])
            send(w_ref(far), w_ref(far), sw, w3.at[d], at_z(md(z + way)))
            send(w_ref(far, d), w_ref(far, d), sw, w4.at[d], at_z(md(z + 2 * way)))
            arrived(w_ref(near), w1.at[d])
            w_share(far)
            w_share(near)

    def w_last():
        for d, way in ((0, 1), (1, -1)):
            v = md(z - 3 * way)
            arrived(w_ref(v), w3.at[d])
            w_share(v)
        for d in (0, 1):
            arrived(w_ref(md(z + 4), d), w4.at[d])
        w_share(md(z + 4))

    w_first()

    loads[2].wait()
    loads[3].wait()
    gate = gate_ref[...].astype(F32)
    up = up_ref[...].astype(F32)
    sig = jax.nn.sigmoid(gate)
    activated = gate * sig
    act[...] = activated
    ups[...] = up * (sig * (1.0 + gate * (1.0 - sig)))
    hid[0] = (activated * up).astype(BF)
    send(hid.at[0], hid.at[1], sh, hp, partner)

    def a_ref(v, h):
        return gt.at[v, pl.ds(4 * h, 4), pl.ds(0, 32)]

    def b_ref(v, h):
        return gt.at[pl.ds(4 * h, 4), v, pl.ds(32, 32)]

    def ring(s, h):
        if not (s == 3 and h == 1):
            ra, rb = a_ref(md(y - s), h), b_ref(md(x - s), h)
            if s > 0:
                arrived(ra, a2r.at[s - 1, h])
            send(ra, ra, s2, a2r.at[s, h], at_y(md(y + 1)))
            if s > 0:
                arrived(rb, b2r.at[s - 1, h])
            send(rb, rb, s2, b2r.at[s, h], at_x(md(x + 1)))
        elif s == 3:
            ra, rb = a_ref(md(y - s), h), b_ref(md(x - s), h)
            arrived(ra, a2r.at[s - 1, h])
            arrived(rb, b2r.at[s - 1, h])
        la, lb = a_ref(md(y + s), h), b_ref(md(x + s), h)
        if s > 0:
            arrived(la, a2l.at[s - 1, h])
        if not (s == 3 and h == 0):
            send(la, la, s2, a2l.at[s, h], at_y(md(y - 1)))
        if s > 0:
            arrived(lb, b2l.at[s - 1, h])
        if not (s == 3 and h == 0):
            send(lb, lb, s2, b2l.at[s, h], at_x(md(x - 1)))

    def share(j, yv, xv):
        theirs = gt.at[yv, pl.ds(4 * cp, 4), pl.ds(0, 32)]
        send(theirs, gp.at[yv, slice(None), pl.ds(0, 32)], sp, pa.at[j], partner)

        @pl.when(lax.div(xv, 4) == cp)
        def _():
            send(
                gt.at[slice(None), xv, pl.ds(32, 32)],
                gp.at[slice(None), lax.rem(xv, 4), pl.ds(32, 32)],
                sb,
                pb.at[j],
                partner,
            )

    def reduce(j, yv, xv):
        mine = gp.at[yv, slice(None), pl.ds(0, 32)]
        arrived(mine, pa.at[j])
        total = jnp.dot(
            gt[yv, pl.ds(4 * c, 4), pl.ds(0, 32)].reshape(128, 256),
            hid[0],
            preferred_element_type=F32,
        ) + jnp.dot(
            gp[yv, :, pl.ds(0, 32)].reshape(128, 256),
            hid[1],
            preferred_element_type=F32,
        )
        part[yv, :, pl.ds(0, 32)] = total.astype(BF).reshape(4, 32, 256)
        o = md(yv - z)
        d = lax.div(o, 4)
        toward = at_z(md(z + 1 - 2 * d))
        rows = part.at[yv, slice(None), pl.ds(0, 32)]

        @pl.when(jnp.logical_or(o == 1, o == 7))
        def _():
            send(rows, got.at[d, slice(None), pl.ds(0, 32)], srs, rs, toward)

        @pl.when(jnp.logical_or(o == 3, o == 5))
        def _():
            send(rows, m3.at[d, slice(None), pl.ds(0, 32)], srs, m3a.at[d], toward)

        @pl.when(o == 4)
        def _():
            for e, way in ((0, 1), (1, -1)):
                send(
                    part.at[yv, slice(None), pl.ds(16 * e, 16)],
                    m4.at[e, slice(None), pl.ds(0, 16)],
                    srs,
                    m4a.at[e],
                    at_z(md(z + 2 * way)),
                )

        @pl.when(lax.div(xv, 4) == c)
        def _():
            xi = lax.rem(xv, 4)
            arrived(gp.at[slice(None), xi, pl.ds(32, 32)], pb.at[j])
            total_b = jnp.dot(
                gt[:, xv, pl.ds(32, 32)].reshape(256, 256),
                hid[0],
                preferred_element_type=F32,
            ) + jnp.dot(
                gp[:, xi, pl.ds(32, 32)].reshape(256, 256),
                hid[1],
                preferred_element_type=F32,
            )
            part[:, xi, pl.ds(32, 32)] = total_b.astype(BF).reshape(N, 32, 256)
            for e, way in ((0, 1), (1, -1)):
                send(
                    part.at[md(z + 4), xi, pl.ds(32 + 16 * e, 16)],
                    m4.at[e, xi, pl.ds(16, 16)],
                    srs,
                    m4b.at[e, xi],
                    at_z(md(z + 2 * way)),
                )
                send(
                    part.at[md(z + 3 * way), xi, pl.ds(32, 32)],
                    m3.at[e, xi, pl.ds(32, 32)],
                    srs,
                    m3b.at[e, xi],
                    at_z(md(z + way)),
                )
            for e, way in ((0, 1), (1, -1)):
                send(
                    part.at[md(z + way), xi, pl.ds(32, 32)],
                    got.at[e, xi, pl.ds(32, 32)],
                    srs,
                    rs,
                    at_z(md(z + way)),
                )

    def pass_on(yv, xv):
        o = md(yv - z)

        @pl.when(jnp.logical_or(o == 2, o == 6))
        def _():
            d = lax.div(o, 4)
            arrived(m3.at[d, slice(None), pl.ds(0, 32)], m3a.at[d])
            arrived(m4.at[d, slice(None), pl.ds(0, 16)], m4a.at[d])
            summed = part[yv, :, pl.ds(0, 32)].astype(F32) + m3[
                d, :, pl.ds(0, 32)
            ].astype(F32)
            lower = m4[d, :, pl.ds(0, 16)].astype(F32)
            first = (d == 0).astype(F32)
            summed = summed + jnp.concatenate(
                [lower * first, lower * (1.0 - first)], axis=1
            )
            part[yv, :, pl.ds(0, 32)] = summed.astype(BF)
            send(
                part.at[yv, slice(None), pl.ds(0, 32)],
                got.at[2 + d, slice(None), pl.ds(0, 32)],
                srs,
                rs,
                at_z(yv),
            )

        @pl.when(lax.div(xv, 4) == c)
        def _():
            xi = lax.rem(xv, 4)
            for e, way in ((0, 1), (1, -1)):
                v = md(z + 2 * way)
                arrived(m3.at[e, xi, pl.ds(32, 32)], m3b.at[e, xi])
                arrived(m4.at[e, xi, pl.ds(16, 16)], m4b.at[e, xi])
                for h in (0, 1):
                    at = pl.ds(32 + 16 * h, 16)
                    summed = part[v, xi, at].astype(F32) + m3[e, xi, at].astype(F32)
                    if h == e:
                        summed = summed + m4[e, xi, pl.ds(16, 16)].astype(F32)
                    part[v, xi, at] = summed.astype(BF)
                send(
                    part.at[v, xi, pl.ds(32, 32)],
                    got.at[2 + e, xi, pl.ds(32, 32)],
                    srs,
                    rs,
                    at_z(v),
                )

    for k in range(1, N):
        arrived(gt.at[y, md(x - k), pl.ds(0, 32)], a1.at[k])
        arrived(gt.at[md(y - k), x, pl.ds(32, 32)], b1.at[k])
    spots = [(y, x)]
    for k in (1, 2, 3):
        spots.append((md(y - k), md(x - k)))
        spots.append((md(y + k), md(x + k)))
    spots.append((md(y + 4), md(x + 4)))

    ring(0, 0)
    ring(0, 1)
    share(0, *spots[0])
    arrived(hid.at[1], hp)
    reduce(0, *spots[0])
    ring(1, 0)
    ring(1, 1)
    share(1, *spots[1])
    share(2, *spots[2])
    w_second()
    reduce(1, *spots[1])
    reduce(2, *spots[2])
    ring(2, 0)
    ring(2, 1)
    share(3, *spots[3])
    share(4, *spots[4])
    reduce(3, *spots[3])
    reduce(4, *spots[4])
    ring(3, 0)
    ring(3, 1)
    share(5, *spots[5])
    share(6, *spots[6])
    w_last()
    reduce(5, *spots[5])
    reduce(6, *spots[6])
    arrived(a_ref(md(y + 4), 0), a2r.at[3, 0])
    arrived(a_ref(md(y + 4), 1), a2l.at[3, 1])
    arrived(b_ref(md(x + 4), 0), b2r.at[3, 0])
    arrived(b_ref(md(x + 4), 1), b2l.at[3, 1])
    share(7, *spots[7])
    reduce(7, *spots[7])
    pass_on(*spots[0])
    pass_on(*spots[1])
    pass_on(*spots[2])
    pass_on(*spots[3])
    pass_on(*spots[4])
    pass_on(*spots[5])
    pass_on(*spots[6])
    arrived(wf.at[slice(None), cp], wp)

    hg[...] = jnp.zeros_like(hg)

    @pl.loop(0, N)
    def _(v):
        both = gt[v].reshape(512, 256)
        hg[...] += lax.dot_general(
            both,
            wf[v].reshape(512, 256),
            (((0,), (0,)), ((), ())),
            preferred_element_type=F32,
        )

    pass_on(*spots[7])
    ugrad_ref[...] = (hg[...] * act[...]).astype(BF)
    ggrad_ref[...] = (hg[...] * ups[...]).astype(BF)

    own = jnp.dot(
        gt[z, pl.ds(4 * c, 4)].reshape(256, 256), hid[0], preferred_element_type=F32
    ) + jnp.dot(gp[z].reshape(256, 256), hid[1], preferred_element_type=F32)

    arrived(gt.at[slice(0, 7), slice(0, 1)], s1)
    arrived(gt.at[slice(0, 7)], s2)
    arrived(gp.at[slice(None), slice(None), pl.ds(0, 32)], sp)
    arrived(gp.at[slice(None), slice(None), pl.ds(32, 32)], sb)
    arrived(wf.at[slice(0, 7), 0], sw)
    arrived(wf.at[slice(None), 0], swp)
    arrived(hid.at[0], sh)
    arrived(part.at[slice(0, 7)], srs)
    arrived(got, rs)
    total = own
    for k in range(4):
        total = total + got[k].reshape(256, 256).astype(F32)
    wgrad_ref[...] = (total * (1.0 / 64.0)).astype(BF)


def store(gg_ref, ug_ref, wg_ref, gg_hbm, ug_hbm, wg_hbm, sem):
    copies = [
        pltpu.make_async_copy(gg_ref, gg_hbm, sem.at[0]),
        pltpu.make_async_copy(ug_ref, ug_hbm, sem.at[1]),
        pltpu.make_async_copy(wg_ref, wg_hbm, sem.at[2]),
    ]
    for copy in copies:
        copy.start()
    for copy in copies:
        copy.wait()


def per_device(gate_pre, up_pre, down_t, grad_out):
    vmem = pl.BlockSpec(memory_space=pltpu.VMEM)
    hbm = pl.BlockSpec(memory_space=pltpu.HBM)
    block = jax.ShapeDtypeStruct((256, 256), BF)
    dma = pltpu.SemaphoreType.DMA
    results = pl.pallas_call(
        kernel,
        out_shape=(block, block, block),
        in_specs=[hbm] * 4,
        out_specs=(vmem, vmem, vmem),
        scratch_shapes=[
            pltpu.VMEM((N, N, 64, 256), BF),
            pltpu.VMEM((N, 4, 64, 256), BF),
            pltpu.VMEM((N, 2, 256, 256), BF),
            pltpu.VMEM((2, 256, 256), BF),
            pltpu.VMEM((256, 256), F32),
            pltpu.VMEM((256, 256), F32),
            pltpu.VMEM((N, 4, 64, 256), BF),
            pltpu.VMEM((4, 4, 64, 256), BF),
            pltpu.VMEM((2, 4, 64, 256), BF),
            pltpu.VMEM((2, 4, 32, 256), BF),
            pltpu.VMEM((256, 256), F32),
            pltpu.VMEM((256, 256), BF),
            pltpu.VMEM((256, 256), BF),
            dma((N,)),
            dma((N,)),
            dma((4, 2)),
            dma((4, 2)),
            dma((4, 2)),
            dma((4, 2)),
            dma((N,)),
            dma((N,)),
            dma((2,)),
            dma((2,)),
            dma((2,)),
            dma((2,)),
            dma,
            dma,
            dma,
            dma((2,)),
            dma((2,)),
            dma((2, 4)),
            dma((2, 4)),
            dma,
            dma,
            dma,
            dma,
            dma,
            dma,
            dma,
            dma,
            dma((4,)),
        ],
        compiler_params=pltpu.CompilerParams(
            collective_id=0, has_side_effects=True, vmem_limit_bytes=56130000
        ),
    )(
        gate_pre,
        up_pre,
        down_t,
        pltpu.with_memory_space_constraint(grad_out.T, pltpu.HBM),
    )
    return pl.pallas_call(
        store,
        out_shape=(block, block, block),
        in_specs=[vmem] * 3,
        out_specs=(hbm, hbm, hbm),
        scratch_shapes=[dma((3,))],
        compiler_params=pltpu.CompilerParams(vmem_limit_bytes=1 << 20),
    )(*results)


def solution(mesh):
    spec = P("row", "col")
    return jax.shard_map(
        per_device,
        mesh=mesh,
        in_specs=(spec, spec, spec, spec),
        out_specs=(spec, spec, spec),
        check_vma=False,
    )
```

```python
import jax
import jax.numpy as jnp
from jax import lax
from jax.experimental import pallas as pl
from jax.experimental.pallas import tpu as pltpu
from jax.sharding import PartitionSpec as P

N = 8
BF = jnp.bfloat16
F32 = jnp.float32


def md(v):
    return lax.rem(v + 2 * N, N)


def kernel(
    gate_hbm,
    up_hbm,
    down_hbm,
    go_hbm,
    ggrad_ref,
    ugrad_ref,
    wgrad_ref,
    gt,
    gp,
    wf,
    hid,
    act,
    ups,
    part,
    got,
    m3,
    m4,
    hg,
    gate_ref,
    up_ref,
    a1,
    b1,
    a2r,
    a2l,
    b2r,
    b2l,
    pa,
    pb,
    w1,
    w2,
    w3,
    w4,
    wp,
    hp,
    rs,
    m3a,
    m4a,
    m3b,
    m4b,
    s1,
    s2,
    sp,
    sb,
    sw,
    swp,
    sh,
    srs,
    loc,
):
    row, col = lax.axis_index("row"), lax.axis_index("col")
    z, c = lax.div(row, 2), lax.rem(row, 2)
    y, x = lax.div(col, N), lax.rem(col, N)
    cp = 1 - c

    def at_x(v):
        return {"row": row, "col": y * N + v}

    def at_y(v):
        return {"row": row, "col": v * N + x}

    def at_z(v):
        return {"row": v * 2 + c, "col": col}

    partner = {"row": z * 2 + cp, "col": col}

    def send(ref, dst, ssem, rsem, dev):
        pltpu.make_async_remote_copy(
            src_ref=ref, dst_ref=dst, send_sem=ssem, recv_sem=rsem, device_id=dev
        ).start()

    def arrived(ref, sem):
        pltpu.make_async_copy(ref, ref, sem).wait()

    barrier = pltpu.get_barrier_semaphore()
    for k in (4, 3, 5, 2, 6, 1, 7):
        pl.semaphore_signal(barrier, inc=1, device_id=at_x(md(x + k)))
        pl.semaphore_signal(barrier, inc=1, device_id=at_y(md(y + k)))
        if k in (1, 2, 6, 7):
            pl.semaphore_signal(barrier, inc=1, device_id=at_z(md(z + k)))
    pl.semaphore_signal(barrier, inc=1, device_id=partner)

    loads = [
        pltpu.make_async_copy(go_hbm, gt.at[y, x], loc.at[0]),
        pltpu.make_async_copy(down_hbm, wf.at[z, c], loc.at[1]),
        pltpu.make_async_copy(gate_hbm, gate_ref, loc.at[2]),
        pltpu.make_async_copy(up_hbm, up_ref, loc.at[3]),
    ]
    for load in loads:
        load.start()
    loads[0].wait()
    loads[1].wait()

    pl.semaphore_wait(barrier, 2 * (N - 1) + 5)

    own_a = gt.at[y, x, pl.ds(0, 32)]
    own_b = gt.at[y, x, pl.ds(32, 32)]
    for k in (4, 3, 5, 2, 6, 1, 7):
        send(own_a, own_a, s1, a1.at[k], at_x(md(x + k)))
        send(own_b, own_b, s1, b1.at[k], at_y(md(y + k)))

    def w_ref(v, half=None):
        return wf.at[v, c] if half is None else wf.at[v, c, pl.ds(128 * half, 128)]

    def w_share(v):
        send(w_ref(v), w_ref(v), swp, wp, partner)

    def w_first():
        mine = w_ref(z)
        for d, way in ((0, 1), (1, -1)):
            send(mine, mine, sw, w2.at[d], at_z(md(z + 2 * way)))
            send(mine, mine, sw, w1.at[d], at_z(md(z + way)))
        w_share(z)

    def w_second():
        for d, way in ((0, 1), (1, -1)):
            near, far = md(z - way), md(z - 2 * way)
            arrived(w_ref(far), w2.at[d])
            send(w_ref(far), w_ref(far), sw, w3.at[d], at_z(md(z + way)))
            send(w_ref(far, d), w_ref(far, d), sw, w4.at[d], at_z(md(z + 2 * way)))
            arrived(w_ref(near), w1.at[d])
            w_share(far)
            w_share(near)

    def w_last():
        for d, way in ((0, 1), (1, -1)):
            v = md(z - 3 * way)
            arrived(w_ref(v), w3.at[d])
            w_share(v)
        for d in (0, 1):
            arrived(w_ref(md(z + 4), d), w4.at[d])
        w_share(md(z + 4))

    w_first()

    loads[2].wait()
    loads[3].wait()
    gate = gate_ref[...].astype(F32)
    up = up_ref[...].astype(F32)
    sig = jax.nn.sigmoid(gate)
    activated = gate * sig
    act[...] = activated
    ups[...] = up * (sig * (1.0 + gate * (1.0 - sig)))
    hid[0] = (activated * up).astype(BF)
    send(hid.at[0], hid.at[1], sh, hp, partner)

    def a_ref(v, h):
        return gt.at[v, pl.ds(4 * h, 4), pl.ds(0, 32)]

    def b_ref(v, h):
        return gt.at[pl.ds(4 * h, 4), v, pl.ds(32, 32)]

    def ring(s, h):
        if not (s == 3 and h == 1):
            ra, rb = a_ref(md(y - s), h), b_ref(md(x - s), h)
            if s > 0:
                arrived(ra, a2r.at[s - 1, h])
            send(ra, ra, s2, a2r.at[s, h], at_y(md(y + 1)))
            if s > 0:
                arrived(rb, b2r.at[s - 1, h])
            send(rb, rb, s2, b2r.at[s, h], at_x(md(x + 1)))
        elif s == 3:
            ra, rb = a_ref(md(y - s), h), b_ref(md(x - s), h)
            arrived(ra, a2r.at[s - 1, h])
            arrived(rb, b2r.at[s - 1, h])
        la, lb = a_ref(md(y + s), h), b_ref(md(x + s), h)
        if s > 0:
            arrived(la, a2l.at[s - 1, h])
        if not (s == 3 and h == 0):
            send(la, la, s2, a2l.at[s, h], at_y(md(y - 1)))
        if s > 0:
            arrived(lb, b2l.at[s - 1, h])
        if not (s == 3 and h == 0):
            send(lb, lb, s2, b2l.at[s, h], at_x(md(x - 1)))

    def share(j, yv, xv):
        theirs = gt.at[yv, pl.ds(4 * cp, 4), pl.ds(0, 32)]
        send(theirs, gp.at[yv, slice(None), pl.ds(0, 32)], sp, pa.at[j], partner)

        @pl.when(lax.div(xv, 4) == cp)
        def _():
            send(
                gt.at[slice(None), xv, pl.ds(32, 32)],
                gp.at[slice(None), lax.rem(xv, 4), pl.ds(32, 32)],
                sb,
                pb.at[j],
                partner,
            )

    def reduce(j, yv, xv):
        mine = gp.at[yv, slice(None), pl.ds(0, 32)]
        arrived(mine, pa.at[j])
        total = jnp.dot(
            gt[yv, pl.ds(4 * c, 4), pl.ds(0, 32)].reshape(128, 256),
            hid[0],
            preferred_element_type=F32,
        ) + jnp.dot(
            gp[yv, :, pl.ds(0, 32)].reshape(128, 256),
            hid[1],
            preferred_element_type=F32,
        )
        part[yv, :, pl.ds(0, 32)] = total.astype(BF).reshape(4, 32, 256)
        o = md(yv - z)
        d = lax.div(o, 4)
        toward = at_z(md(z + 1 - 2 * d))
        rows = part.at[yv, slice(None), pl.ds(0, 32)]

        @pl.when(jnp.logical_or(o == 1, o == 7))
        def _():
            send(rows, got.at[d, slice(None), pl.ds(0, 32)], srs, rs, toward)

        @pl.when(jnp.logical_or(o == 3, o == 5))
        def _():
            send(rows, m3.at[d, slice(None), pl.ds(0, 32)], srs, m3a.at[d], toward)

        @pl.when(o == 4)
        def _():
            for e, way in ((0, 1), (1, -1)):
                send(
                    part.at[yv, slice(None), pl.ds(16 * e, 16)],
                    m4.at[e, slice(None), pl.ds(0, 16)],
                    srs,
                    m4a.at[e],
                    at_z(md(z + 2 * way)),
                )

        @pl.when(lax.div(xv, 4) == c)
        def _():
            xi = lax.rem(xv, 4)
            arrived(gp.at[slice(None), xi, pl.ds(32, 32)], pb.at[j])
            total_b = jnp.dot(
                gt[:, xv, pl.ds(32, 32)].reshape(256, 256),
                hid[0],
                preferred_element_type=F32,
            ) + jnp.dot(
                gp[:, xi, pl.ds(32, 32)].reshape(256, 256),
                hid[1],
                preferred_element_type=F32,
            )
            part[:, xi, pl.ds(32, 32)] = total_b.astype(BF).reshape(N, 32, 256)
            for e, way in ((0, 1), (1, -1)):
                send(
                    part.at[md(z + 4), xi, pl.ds(32 + 16 * e, 16)],
                    m4.at[e, xi, pl.ds(16, 16)],
                    srs,
                    m4b.at[e, xi],
                    at_z(md(z + 2 * way)),
                )
                send(
                    part.at[md(z + 3 * way), xi, pl.ds(32, 32)],
                    m3.at[e, xi, pl.ds(32, 32)],
                    srs,
                    m3b.at[e, xi],
                    at_z(md(z + way)),
                )
            for e, way in ((0, 1), (1, -1)):
                send(
                    part.at[md(z + way), xi, pl.ds(32, 32)],
                    got.at[e, xi, pl.ds(32, 32)],
                    srs,
                    rs,
                    at_z(md(z + way)),
                )

    def pass_on(yv, xv):
        o = md(yv - z)

        @pl.when(jnp.logical_or(o == 2, o == 6))
        def _():
            d = lax.div(o, 4)
            arrived(m3.at[d, slice(None), pl.ds(0, 32)], m3a.at[d])
            arrived(m4.at[d, slice(None), pl.ds(0, 16)], m4a.at[d])
            summed = part[yv, :, pl.ds(0, 32)].astype(F32) + m3[
                d, :, pl.ds(0, 32)
            ].astype(F32)
            lower = m4[d, :, pl.ds(0, 16)].astype(F32)
            first = (d == 0).astype(F32)
            summed = summed + jnp.concatenate(
                [lower * first, lower * (1.0 - first)], axis=1
            )
            part[yv, :, pl.ds(0, 32)] = summed.astype(BF)
            send(
                part.at[yv, slice(None), pl.ds(0, 32)],
                got.at[2 + d, slice(None), pl.ds(0, 32)],
                srs,
                rs,
                at_z(yv),
            )

        @pl.when(lax.div(xv, 4) == c)
        def _():
            xi = lax.rem(xv, 4)
            for e, way in ((0, 1), (1, -1)):
                v = md(z + 2 * way)
                arrived(m3.at[e, xi, pl.ds(32, 32)], m3b.at[e, xi])
                arrived(m4.at[e, xi, pl.ds(16, 16)], m4b.at[e, xi])
                for h in (0, 1):
                    at = pl.ds(32 + 16 * h, 16)
                    summed = part[v, xi, at].astype(F32) + m3[e, xi, at].astype(F32)
                    if h == e:
                        summed = summed + m4[e, xi, pl.ds(16, 16)].astype(F32)
                    part[v, xi, at] = summed.astype(BF)
                send(
                    part.at[v, xi, pl.ds(32, 32)],
                    got.at[2 + e, xi, pl.ds(32, 32)],
                    srs,
                    rs,
                    at_z(v),
                )

    for k in range(1, N):
        arrived(gt.at[y, md(x - k), pl.ds(0, 32)], a1.at[k])
        arrived(gt.at[md(y - k), x, pl.ds(32, 32)], b1.at[k])
    spots = [(y, x)]
    for k in (1, 2, 3):
        spots.append((md(y - k), md(x - k)))
        spots.append((md(y + k), md(x + k)))
    spots.append((md(y + 4), md(x + 4)))

    ring(0, 0)
    ring(0, 1)
    share(0, *spots[0])
    arrived(hid.at[1], hp)
    reduce(0, *spots[0])
    ring(1, 0)
    ring(1, 1)
    share(1, *spots[1])
    share(2, *spots[2])
    w_second()
    reduce(1, *spots[1])
    reduce(2, *spots[2])
    ring(2, 0)
    ring(2, 1)
    share(3, *spots[3])
    share(4, *spots[4])
    reduce(3, *spots[3])
    reduce(4, *spots[4])
    ring(3, 0)
    ring(3, 1)
    share(5, *spots[5])
    share(6, *spots[6])
    w_last()
    reduce(5, *spots[5])
    reduce(6, *spots[6])
    arrived(a_ref(md(y + 4), 0), a2r.at[3, 0])
    arrived(a_ref(md(y + 4), 1), a2l.at[3, 1])
    arrived(b_ref(md(x + 4), 0), b2r.at[3, 0])
    arrived(b_ref(md(x + 4), 1), b2l.at[3, 1])
    share(7, *spots[7])
    reduce(7, *spots[7])
    pass_on(*spots[0])
    pass_on(*spots[1])
    pass_on(*spots[2])
    pass_on(*spots[3])
    pass_on(*spots[4])
    pass_on(*spots[5])
    pass_on(*spots[6])
    arrived(wf.at[slice(None), cp], wp)

    hg[...] = jnp.zeros_like(hg)

    @pl.loop(0, N)
    def _(v):
        both = gt[v].reshape(512, 256)
        hg[...] += lax.dot_general(
            both,
            wf[v].reshape(512, 256),
            (((0,), (0,)), ((), ())),
            preferred_element_type=F32,
        )

    pass_on(*spots[7])
    ugrad_ref[...] = (hg[...] * act[...]).astype(BF)
    ggrad_ref[...] = (hg[...] * ups[...]).astype(BF)

    own = jnp.dot(
        gt[z, pl.ds(4 * c, 4)].reshape(256, 256), hid[0], preferred_element_type=F32
    ) + jnp.dot(gp[z].reshape(256, 256), hid[1], preferred_element_type=F32)

    arrived(got, rs)
    total = own
    for k in range(4):
        total = total + got[k].reshape(256, 256).astype(F32)
    wgrad_ref[...] = (total * (1.0 / 64.0)).astype(BF)
    arrived(gt.at[slice(0, 7), slice(0, 1)], s1)
    arrived(gt.at[slice(0, 7)], s2)
    arrived(gp.at[slice(None), slice(None), pl.ds(0, 32)], sp)
    arrived(gp.at[slice(None), slice(None), pl.ds(32, 32)], sb)
    arrived(wf.at[slice(0, 7), 0], sw)
    arrived(wf.at[slice(None), 0], swp)
    arrived(hid.at[0], sh)
    arrived(part.at[slice(0, 7)], srs)


def store(gg_ref, ug_ref, wg_ref, gg_hbm, ug_hbm, wg_hbm, sem):
    copies = [
        pltpu.make_async_copy(gg_ref, gg_hbm, sem.at[0]),
        pltpu.make_async_copy(ug_ref, ug_hbm, sem.at[1]),
        pltpu.make_async_copy(wg_ref, wg_hbm, sem.at[2]),
    ]
    for copy in copies:
        copy.start()
    for copy in copies:
        copy.wait()


def per_device(gate_pre, up_pre, down_t, grad_out):
    vmem = pl.BlockSpec(memory_space=pltpu.VMEM)
    hbm = pl.BlockSpec(memory_space=pltpu.HBM)
    block = jax.ShapeDtypeStruct((256, 256), BF)
    dma = pltpu.SemaphoreType.DMA
    results = pl.pallas_call(
        kernel,
        out_shape=(block, block, block),
        in_specs=[hbm] * 4,
        out_specs=(vmem, vmem, vmem),
        scratch_shapes=[
            pltpu.VMEM((N, N, 64, 256), BF),
            pltpu.VMEM((N, 4, 64, 256), BF),
            pltpu.VMEM((N, 2, 256, 256), BF),
            pltpu.VMEM((2, 256, 256), BF),
            pltpu.VMEM((256, 256), F32),
            pltpu.VMEM((256, 256), F32),
            pltpu.VMEM((N, 4, 64, 256), BF),
            pltpu.VMEM((4, 4, 64, 256), BF),
            pltpu.VMEM((2, 4, 64, 256), BF),
            pltpu.VMEM((2, 4, 32, 256), BF),
            pltpu.VMEM((256, 256), F32),
            pltpu.VMEM((256, 256), BF),
            pltpu.VMEM((256, 256), BF),
            dma((N,)),
            dma((N,)),
            dma((4, 2)),
            dma((4, 2)),
            dma((4, 2)),
            dma((4, 2)),
            dma((N,)),
            dma((N,)),
            dma((2,)),
            dma((2,)),
            dma((2,)),
            dma((2,)),
            dma,
            dma,
            dma,
            dma((2,)),
            dma((2,)),
            dma((2, 4)),
            dma((2, 4)),
            dma,
            dma,
            dma,
            dma,
            dma,
            dma,
            dma,
            dma,
            dma((4,)),
        ],
        compiler_params=pltpu.CompilerParams(
            collective_id=0, has_side_effects=True, vmem_limit_bytes=56130000
        ),
    )(
        gate_pre,
        up_pre,
        down_t,
        pltpu.with_memory_space_constraint(grad_out.T, pltpu.HBM),
    )
    return pl.pallas_call(
        store,
        out_shape=(block, block, block),
        in_specs=[vmem] * 3,
        out_specs=(hbm, hbm, hbm),
        scratch_shapes=[dma((3,))],
        compiler_params=pltpu.CompilerParams(vmem_limit_bytes=1 << 20),
    )(*results)


def solution(mesh):
    spec = P("row", "col")
    return jax.shard_map(
        per_device,
        mesh=mesh,
        in_specs=(spec, spec, spec, spec),
        out_specs=(spec, spec, spec),
        check_vma=False,
    )
```
